256 devices in a mesh: tm: 16 (over z, x_lo), gx: 8 (over y, core), gy: 2 (over x_hi).
Axes of the slice: x: 4 (x_hi: 2, x_lo: 2; x = x_hi * 2 + x_lo), y: 4, z: 8, core: 2. Of those that a mesh axis runs over, the one named last changes fastest.
Arguments:
- start_field: float32 [3, 4, 512, 512], P(None, None, 'gx', 'gy'), may hold values from -1 to 1, as said below
- demag_field: float32 [3, 4, 512, 512], P(None, None, 'gx', 'gy'), may hold values from -3 to 3
- region_map: int32 [4, 512, 512], P(None, 'gx', 'gy'), may hold values from 0 to 3
- material_table: float32 [4, 3], replicated, may hold values from 0.3 to 1.2
Outputs:
- end_states: float32 [16, 3, 4, 512, 512], P('tm', None, None, 'gx', 'gy')
- predicted_states: float32 [16, 3, 4, 512, 512], P('tm', None, None, 'gx', 'gy')
The draws below stay inside these ranges and needn't reach their ends.
Inputs may be any that keep to these rules, and one draw needn't show every extreme that they name: `start_field`: every cell's vector has length at most 1.
All inputs are finite; a program needn't handle non-finite values.
Results may differ from the reference program's by a relative error of at most 0.00002.
Values sent between devices are 32-bit elements; how exact they have to be, the bound alone decides.
A program may use at most 64 MiB of HBM per device.

```python
import jax
import jax.numpy as jnp
from jax import lax

Z = 4
ITERS = 4
CLASSES = 4
SLICES = 16
NX = 512
NY = 512


def draw_start_field(key, part):
    vectors = jax.random.normal(key, (3, Z, NX, NY), jnp.float32)
    length = jnp.sqrt(jnp.sum(vectors * vectors, axis=0, keepdims=True) + 0.01)
    return vectors / length


def plant(values, stream_key, low, top_value):
    place = [jax.random.randint(jax.random.fold_in(stream_key, axis), (), 0, length) for axis, length in enumerate(values.shape)]
    widest = values.shape.index(max(values.shape))
    beside = place[:widest] + [(place[widest] + 1) % values.shape[widest]] + place[widest + 1:]
    return values.at[tuple(place)].set(low).at[tuple(beside)].set(top_value)


def level_of(own_key, shape, pieces, least, high):
    def one(axis_at, blocks):
        heights = jax.random.uniform(jax.random.fold_in(jax.random.fold_in(own_key, 6), axis_at), (blocks,), jnp.float32, least / len(pieces), high / len(pieces))
        return jnp.repeat(jnp.exp(heights), shape[axis_at] // blocks).reshape((-1,) + (1,) * (len(shape) - axis_at - 1))

    gain = one(*pieces[0])
    for cut in pieces[1:]:
        gain = gain * one(*cut)
    return gain


def noise(stream_key, dims, spread, reach, shards=(), kind=jnp.bfloat16):
    level = level_of(stream_key, dims, shards, -0.22, 0.18) if shards else 1.0
    values = jax.random.normal(stream_key, dims, jnp.float32) * spread * level
    return jnp.minimum(jnp.maximum(values, -reach), reach).astype(kind)


def setup_inputs(seed: int = 0) -> dict:
    seeds = jax.random.split(jax.random.key(seed), 5)
    return {
        "start_field": draw_start_field(jax.random.fold_in(seeds[4], 71), 0),
        "demag_field": noise(seeds[1], (3, Z, NX, NY), 0.5, 3.0, ((2, 8), (3, 2)), jnp.float32),
        "region_map": plant(jax.random.randint(seeds[2], (Z, NX, NY), 0, CLASSES), jax.random.fold_in(seeds[2], 1), 0, CLASSES - 1).astype(jnp.int32),
        "material_table": jnp.clip(jax.random.uniform(seeds[3], (CLASSES, 3), jnp.float32, 0.3, 1.2), 0.3, 1.2),
    }


damping = 0.5
slice_length = 0.05


def cross(left, right):
    return jnp.stack([left[1] * right[2] - left[2] * right[1],
                      left[2] * right[0] - left[0] * right[2],
                      left[0] * right[1] - left[1] * right[0]])


def rate(center, x_next, x_prev, y_next, y_prev, exchange, chirality, anisotropy, demag):
    z_next = jnp.concatenate([center[:, 1:], center[:, -1:]], axis=1)
    z_prev = jnp.concatenate([center[:, :1], center[:, :-1]], axis=1)
    laplace = x_next + x_prev + y_next + y_prev + z_next + z_prev - 6.0 * center
    slope_x = 0.5 * (x_next - x_prev)
    slope_y = 0.5 * (y_next - y_prev)
    field_x = exchange * laplace[0] + chirality * slope_x[2] + demag[0]
    field_y = exchange * laplace[1] + chirality * slope_y[2] + demag[1]
    field_z = exchange * laplace[2] - chirality * (slope_x[0] + slope_y[1]) + 2.0 * anisotropy * center[2] + demag[2]
    field = jnp.stack([field_x, field_y, field_z])
    torque = cross(center, field)
    return -torque - damping * cross(center, torque)


def whole_rate(magnet, exchange, chirality, anisotropy, demag):
    return rate(magnet, jnp.roll(magnet, -1, 2), jnp.roll(magnet, 1, 2),
                jnp.roll(magnet, -1, 3), jnp.roll(magnet, 1, 3),
                exchange, chirality, anisotropy, demag)


def reference(start_field, demag_field, region_map, material_table):
    looked = material_table[region_map]
    exchange = looked[..., 0]
    chirality = looked[..., 1]
    anisotropy = looked[..., 2]
    half = 0.5 * slice_length

    def evaluate(magnet):
        return whole_rate(magnet, exchange, chirality, anisotropy, demag_field)

    def predict(current, unused):
        advanced = current + slice_length * evaluate(current)
        return advanced, advanced

    def sweep(packed):
        begin, nodes, rates = packed
        rate_zero = evaluate(begin)
        node_one = begin + half * (rate_zero - rates[0]) + slice_length * (
            (5.0 / 24.0) * rates[0] + (1.0 / 3.0) * rates[1] - (1.0 / 24.0) * rates[2])
        rate_one = evaluate(node_one)
        node_two = node_one + half * (rate_one - rates[1]) + slice_length * (
            (-1.0 / 24.0) * rates[0] + (1.0 / 3.0) * rates[1] + (5.0 / 24.0) * rates[2])
        rate_two = evaluate(node_two)
        return (jnp.stack([begin, node_one, node_two]), jnp.stack([rate_zero, rate_one, rate_two]))

    final_guess, later = lax.scan(predict, start_field, None, length=SLICES - 1)
    begins = jnp.concatenate([start_field[None], later], axis=0)
    first_rates = lax.map(evaluate, begins)
    nodes = jnp.broadcast_to(begins[:, None], (SLICES, 3) + start_field.shape)
    rates = jnp.broadcast_to(first_rates[:, None], (SLICES, 3) + start_field.shape)
    for sweep_index in range(ITERS):
        if sweep_index == 0:
            starts = begins
        else:
            starts = jnp.concatenate([start_field[None], nodes[:-1, 2]], axis=0)
        nodes, rates = lax.map(sweep, (starts, nodes, rates))
    return nodes[:, 2], begins
```

```python
import jax
import jax.numpy as jnp
from jax import lax
from jax.experimental import pallas as pl
from jax.experimental.pallas import tpu as pltpu
from jax.sharding import PartitionSpec as P

ITERS = 4
HALO = 23
STEP = 0.05
DEPTH = 8
TOP = 32
ROWS = 128
SHIFT = 87


def halo_rows(halo, body):
    first = (TOP - halo) // 8
    last = (TOP + 64 + halo + 7) // 8

    def run(block, carry):
        body(pl.multiple_of(block * 8, 8))
        return carry

    lax.fori_loop(first, last, run, 0)


def rates(field, coeffs, row, part):
    exchange_ref, slope_ref, axis_ref, demag_ref = coeffs
    rows = pl.ds(row, 8)
    above = pl.ds(row - 1, 8)
    below = pl.ds(row + 1, 8)
    cells = [[field[c, z, part, rows, :] for z in range(4)] for c in range(3)]
    out = []
    for z in range(4):
        sums = []
        slope_x = [None] * 3
        slope_y = [None] * 3
        for c in range(3):
            center = cells[c][z]
            x_next = field[c, z, part, below, :]
            x_prev = field[c, z, part, above, :]
            y_next = pltpu.roll(center, 127, 1)
            y_prev = pltpu.roll(center, 1, 1)
            z_pair = cells[c][min(z + 1, 3)] + cells[c][max(z - 1, 0)]
            sums.append((x_next + x_prev) + (y_next + y_prev) + z_pair)
            if c != 1:
                slope_x[c] = x_next - x_prev
            if c != 0:
                slope_y[c] = y_next - y_prev
        mx, my, mz = (cells[c][z] for c in range(3))
        exchange = exchange_ref[z, part, rows, :]
        slope = slope_ref[z, part, rows, :]
        axis = axis_ref[z, part, rows, :]
        hx = exchange * (sums[0] - 6.0 * mx) + slope * slope_x[2] + demag_ref[0, z, part, rows, :]
        hy = exchange * (sums[1] - 6.0 * my) + slope * slope_y[2] + demag_ref[1, z, part, rows, :]
        hz = exchange * sums[2] + axis * mz - slope * (slope_x[0] + slope_y[1]) + demag_ref[2, z, part, rows, :]
        ax, ay, az = 0.5 * mx, 0.5 * my, 0.5 * mz
        gx = hx + (ay * hz - az * hy)
        gy = hy + (az * hx - ax * hz)
        gz = hz + (ax * hy - ay * hx)
        out.append((gy * mz - gz * my, gz * mx - gx * mz, gx * my - gy * mx))
    return out, cells


def compute_kernel(index_ref, start_hbm, demag_ref, exchange_ref, slope_ref, axis_ref, end_ref, guess_ref,
                   state, node_one, extra, rate_zero, rate_one, rate_two, node_two, sem):
    me = index_ref[0]
    coeffs = (exchange_ref, slope_ref, axis_ref, demag_ref)
    copy = pltpu.make_async_copy(start_hbm, state.at[0], sem)
    copy.start()
    copy.wait()

    def put(ref, lead, z, part, row, values):
        for c in range(3):
            ref[(*lead, c, z, part, pl.ds(row, 8), slice(None))] = values[c]

    def get(ref, lead, z, part, row):
        return [ref[(*lead, c, z, part, pl.ds(row, 8), slice(None))] for c in range(3)]

    def assemble(field, out_ref):
        lane = lax.broadcasted_iota(jnp.int32, (8, 128), 1)

        def body(block, carry):
            row = pl.multiple_of(block * 8, 8)
            for c in range(3):
                for z in range(4):
                    a, b, d = (field[c, z, part, pl.ds(row + TOP, 8), :] for part in range(3))
                    out_ref[c, z, pl.ds(row, 8), 0:128] = jnp.where(lane < 84, pltpu.roll(a, 128 - 23, 1), pltpu.roll(b, 64, 1))
                    out_ref[c, z, pl.ds(row, 8), 128:256] = jnp.where(lane < 43, pltpu.roll(b, 64, 1), pltpu.roll(d, 23, 1))
            return carry

        lax.fori_loop(0, 8, body, 0)

    def slot_of(step):
        return jnp.where(step == 0, 0, 1 + lax.rem(step + 1, 2))

    def advance(step, carry):
        source = state.at[slot_of(step)]
        target = state.at[slot_of(step + 1)]
        halo = me - step + DEPTH - 1

        @pl.when(step < me - 3)
        def _():
            def body(row):
                for part in range(3):
                    out, cells = rates(source, coeffs, row, part)
                    for z in range(4):
                        put(target, (), z, part, row, [cells[c][z] + out[z][c] for c in range(3)])

            halo_rows(halo, body)

        @pl.when(step >= me - 3)
        def _():
            kept = step - me + 3

            def body(row):
                for part in range(3):
                    out, cells = rates(source, coeffs, row, part)
                    for z in range(4):
                        put(target, (), z, part, row, [cells[c][z] + out[z][c] for c in range(3)])
                        put(rate_zero, (kept,), z, part, row, out[z])
                        put(node_one, (kept,), z, part, row, [cells[c][z] + 0.5 * out[z][c] for c in range(3)])

            halo_rows(halo, body)

        @pl.when((step == 7) & (me > 12))
        def _():
            lane = lax.broadcasted_iota(jnp.int32, (8, 128), 1)

            def body(row):
                for c in range(3):
                    for z in range(4):
                        a, b, d = (target[c, z, part, pl.ds(row, 8), :] for part in range(3))
                        target[c, z, 0, pl.ds(row, 8), :] = jnp.where(lane < 107, a, pltpu.roll(b, SHIFT, 1))
                        target[c, z, 1, pl.ds(row, 8), :] = jnp.where(
                            lane < 20, pltpu.roll(a, 128 - SHIFT, 1), jnp.where(lane < 107, b, pltpu.roll(d, SHIFT, 1)))
                        target[c, z, 2, pl.ds(row, 8), :] = jnp.where(lane < 20, pltpu.roll(b, 128 - SHIFT, 1), d)

            halo_rows(halo, body)

        return carry

    lax.fori_loop(0, me + 1, advance, 0)
    assemble(state.at[slot_of(me)], guess_ref)

    for sweep in range(ITERS):
        halo = DEPTH - 2 - 2 * sweep

        def one_slice(count, carry, sweep=sweep, halo=halo):
            kept = 3 - count
            exists = me - count >= 0

            @pl.when(exists)
            def _():
                def body(row):
                    for part in range(3):
                        out, cells = rates(node_one.at[kept], coeffs, row, part)
                        for z in range(4):
                            new = [cells[c][z] + 0.5 * out[z][c] for c in range(3)]
                            if sweep:
                                add = get(extra, (kept,), z, part, row)
                                new = [new[c] + add[c] for c in range(3)]
                            put(node_two, (), z, part, row, new)
                            if sweep + 1 < ITERS:
                                put(rate_one, (kept,), z, part, row, out[z])

                halo_rows(halo, body)

            if sweep + 1 == ITERS:
                return carry

            @pl.when(jnp.logical_not(exists))
            def _():
                def body(row):
                    for part in range(3):
                        for z in range(4):
                            put(node_two, (), z, part, row, get(state, (0,), z, part, row))

                halo_rows(halo, body)

            @pl.when(count == 0)
            def _():
                def body(row):
                    for part in range(3):
                        out, cells = rates(node_two, coeffs, row, part)
                        for z in range(4):
                            put(rate_two, (), z, part, row, out[z])

                halo_rows(halo - 1, body)

            @pl.when(count > 0)
            def _():
                def body(row):
                    for part in range(3):
                        out, cells = rates(node_two, coeffs, row, part)
                        for z in range(4):
                            old = get(rate_zero, (kept + 1,), z, part, row)
                            mid = get(rate_one, (kept + 1,), z, part, row)
                            far = get(rate_two, (), z, part, row)
                            put(node_one, (kept + 1,), z, part, row, [
                                cells[c][z] + 0.5 * out[z][c] + (1.0 / 24.0) * (8.0 * mid[c] - 7.0 * old[c] - far[c])
                                for c in range(3)])
                            put(extra, (kept + 1,), z, part, row, [
                                (1.0 / 24.0) * ((far[c] - old[c]) + 4.0 * (far[c] - mid[c]))
                                for c in range(3)])
                            put(rate_zero, (kept + 1,), z, part, row, out[z])
                            put(rate_two, (), z, part, row, out[z])

                halo_rows(halo - 1, body)

            return carry

        lax.fori_loop(0, ITERS - sweep, one_slice, 0)
    assemble(node_two, end_ref)


def compute(index, start, demag, exchange, slope, axis, interpret=False):
    field = (3, 4, 3, ROWS, 128)
    vmem = pl.BlockSpec(memory_space=pltpu.VMEM)
    return pl.pallas_call(
        compute_kernel,
        name="llg",
        out_shape=[jax.ShapeDtypeStruct((3, 4, 64, 256), jnp.float32)] * 2,
        in_specs=[pl.BlockSpec(memory_space=pltpu.SMEM), pl.BlockSpec(memory_space=pl.ANY)] + [vmem] * 4,
        out_specs=[vmem] * 2,
        scratch_shapes=[
            pltpu.VMEM((3,) + field, jnp.float32),
            pltpu.VMEM((4,) + field, jnp.float32),
            pltpu.VMEM((4,) + field, jnp.float32),
            pltpu.VMEM((4,) + field, jnp.float32),
            pltpu.VMEM((4,) + field, jnp.float32),
            pltpu.VMEM(field, jnp.float32),
            pltpu.VMEM(field, jnp.float32),
            pltpu.SemaphoreType.DMA,
        ],
        compiler_params=pltpu.CompilerParams(vmem_limit_bytes=63 * 1024 * 1024),
        interpret=interpret,
    )(index, start, demag, exchange, slope, axis)


def blocked(padded):
    parts = jnp.stack([padded[..., SHIFT * k:SHIFT * k + 128] for k in range(3)], axis=2)
    edge = TOP - HALO
    return jnp.pad(parts, ((0, 0), (0, 0), (0, 0), (edge, ROWS - edge - padded.shape[2]), (0, 0)))


def coefficients(padded_region, material_table):
    columns = []
    for column in range(3):
        total = jnp.zeros(padded_region.shape, jnp.float32)
        for klass in range(material_table.shape[0]):
            total = total + (padded_region == klass).astype(jnp.float32) * material_table[klass, column]
        columns.append(total)
    exchange = STEP * columns[0]
    return exchange, (0.5 * STEP) * columns[1], (2.0 * STEP) * columns[2] - 6.0 * exchange


def from_padded(index, padded, material_table, interpret=False):
    fields = blocked(padded)
    exchange, slope, axis = coefficients(fields[6], material_table)
    return compute(index, fields[:3], fields[3:6], exchange, slope, axis, interpret)


def on_device(start_field, demag_field, region_map, material_table):
    tile = jnp.concatenate([start_field, STEP * demag_field, region_map.astype(jnp.float32)[None]], axis=0)
    strips = jnp.concatenate([tile[..., :HALO], tile[..., -HALO:]], axis=3)
    pairs = [(2 * t + g, 2 * (t ^ 1) + (g ^ 1)) for t in range(16) for g in range(2)]
    strips = lax.ppermute(strips, ("tm", "gy"), pairs)
    tile = jnp.concatenate([strips[..., HALO:], tile, strips[..., :HALO]], axis=3)
    count = lax.axis_size("gx")
    above = lax.ppermute(tile[:, :, -HALO:], "gx", [(i, (i + 1) % count) for i in range(count)])
    below = lax.ppermute(tile[:, :, :HALO], "gx", [((i + 1) % count, i) for i in range(count)])
    padded = jnp.concatenate([above, tile, below], axis=2)
    index = lax.axis_index("tm").astype(jnp.int32)[None]
    end, guess = from_padded(index, padded, material_table)
    return end[None], guess[None]


def solution(mesh):
    placed = (P(None, None, "gx", "gy"), P(None, None, "gx", "gy"), P(None, "gx", "gy"), P())
    return jax.shard_map(
        on_device,
        mesh=mesh,
        in_specs=placed,
        out_specs=(P("tm", None, None, "gx", "gy"), P("tm", None, None, "gx", "gy")),
        check_vma=False,
    )
```

```python
import jax
import jax.numpy as jnp
from jax import lax
from jax.experimental import pallas as pl
from jax.experimental.pallas import tpu as pltpu
from jax.sharding import PartitionSpec as P

MESH = pl.DeviceIdType.MESH
ITERS = 4
HALO = 24
SIDE = 32
STEP = 0.05
DEPTH = 8
FIRST = 8
LAST = 64
ROWS = 72
PARTS = 5


def blocks_of(halo):
    return (FIRST + HALO - halo) // 8, LAST // 8


def lanes():
    return lax.broadcasted_iota(jnp.int32, (8, 128), 1)


def prepare(field, sum_ref, difference_ref, row):
    rows = pl.ds(row, 8)
    lane = lanes()
    first, last = lane == 0, lane == 127
    for c in range(3):
        for z in range(4):
            v = [field[c, z, part, rows, :] for part in range(PARTS)]
            n = [pltpu.roll(x, 127, 1) for x in v]
            p = [pltpu.roll(x, 1, 1) for x in v]
            following = [
                jnp.where(last, n[1], n[0]),
                jnp.where(last, n[4], n[1]),
                jnp.where(last, n[3], n[2]),
                jnp.where(last, pltpu.roll(v[4], 95, 1), n[3]),
                jnp.where(last, n[0], jnp.where(lane == 95, pltpu.roll(v[2], 95, 1), n[4])),
            ]
            previous = [
                jnp.where(first, p[4], p[0]),
                jnp.where(first, p[0], p[1]),
                jnp.where(first, pltpu.roll(v[4], 33, 1), p[2]),
                jnp.where(first, p[2], p[3]),
                jnp.where(first, p[1], jnp.where(lane == 32, pltpu.roll(v[3], 33, 1), p[4])),
            ]
            for part in range(PARTS):
                sum_ref[c, z, part, rows, :] = following[part] + previous[part]
                if c:
                    difference_ref[c - 1, z, part, rows, :] = following[part] - previous[part]


def join_halves(field):
    lane = lax.broadcasted_iota(jnp.int32, (1, 128), 1)
    down = (lane < 32) | ((lane >= 64) & (lane < 96))
    edge, beyond = pl.ds(LAST - 1, 1), pl.ds(LAST, 1)
    for c in range(3):
        for z in range(4):
            for part in range(4):
                field[c, z, part, beyond, :] = field[c, z, (part + 2) % 4, edge, :]
            side = field[c, z, 4, edge, :]
            field[c, z, 4, beyond, :] = jnp.where(down, pltpu.roll(side, 96, 1), pltpu.roll(side, 32, 1))


def rates(field, aux, row, part):
    exchange_ref, slope_ref, signed_ref, axis_ref, demag_ref, sum_ref, difference_ref = aux
    rows = pl.ds(row, 8)
    above = pl.ds(row - 1, 8)
    below = pl.ds(row + 1, 8)
    cells = [[field[c, z, part, rows, :] for z in range(4)] for c in range(3)]
    out = []
    for z in range(4):
        sums = []
        slope_x = [None] * 3
        for c in range(3):
            x_next = field[c, z, part, below, :]
            x_prev = field[c, z, part, above, :]
            z_pair = cells[c][min(z + 1, 3)] + cells[c][max(z - 1, 0)]
            sums.append((x_next + x_prev) + sum_ref[c, z, part, rows, :] + z_pair)
            if c != 1:
                slope_x[c] = x_next - x_prev
        mx, my, mz = (cells[c][z] for c in range(3))
        exchange = exchange_ref[z, part, rows, :]
        slope = slope_ref[z, part, rows, :]
        signed = signed_ref[z, part, rows, :]
        axis = axis_ref[z, part, rows, :]
        hx = exchange * (sums[0] - 6.0 * mx) + signed * slope_x[2] + demag_ref[0, z, part, rows, :]
        hy = exchange * (sums[1] - 6.0 * my) + slope * difference_ref[1, z, part, rows, :] + demag_ref[1, z, part, rows, :]
        hz = (exchange * sums[2] + axis * mz
              - (signed * slope_x[0] + slope * difference_ref[0, z, part, rows, :]) + demag_ref[2, z, part, rows, :])
        ax, ay, az = 0.5 * mx, 0.5 * my, 0.5 * mz
        gx = hx + (ay * hz - az * hy)
        gy = hy + (az * hx - ax * hz)
        gz = hz + (ax * hy - ay * hx)
        out.append((gy * mz - gz * my, gz * mx - gx * mz, gx * my - gy * mx))
    return out, cells


def put(ref, lead, z, part, row, values):
    for c in range(3):
        ref[(*lead, c, z, part, pl.ds(row, 8), slice(None))] = values[c]


def get(ref, lead, z, part, row):
    return [ref[(*lead, c, z, part, pl.ds(row, 8), slice(None))] for c in range(3)]


def evaluate(field, aux, halo, use):
    first, last = blocks_of(halo)
    join_halves(field)
    prepare(field, aux[5], aux[6], pl.multiple_of(first * 8, 8))

    def run(block, carry):
        row = pl.multiple_of(block * 8, 8)
        prepare(field, aux[5], aux[6], row + 8)
        for part in range(PARTS):
            out, cells = rates(field, aux, row, part)
            use(row, part, out, cells)
        return carry

    lax.fori_loop(first, last, run, 0)


def assemble(field, out_ref):
    upside_down = 7 - lax.broadcasted_iota(jnp.int32, (8, 128), 0)

    def body(block, carry):
        row = pl.multiple_of(block * 8, 8)
        for c in range(3):
            for z in range(4):
                for part in range(2):
                    columns = slice(128 * part, 128 * part + 128)
                    out_ref[c, z, pl.ds(row, 8), columns] = field[c, z, part, pl.ds(FIRST + HALO + row, 8), :]
                    out_ref[c, z, pl.ds(row + 32, 8), columns] = jnp.take_along_axis(
                        field[c, z, part + 2, pl.ds(LAST - 8 - row, 8), :], upside_down, axis=0)
        return carry

    lax.fori_loop(0, 4, body, 0)


def fill_coefficients(table, region, exchange_ref, slope_ref, signed_ref, axis_ref):
    lane = lanes()
    upper_side = (lane < 32) | (lane >= 96)

    def body(block, carry):
        rows = pl.ds(pl.multiple_of(block * 8, 8), 8)
        for z in range(4):
            for part in range(PARTS):
                kind = region[z, part, rows, :]
                exchange, slope, axis = (
                    jnp.where(kind == 0.0, table[0, k], jnp.where(kind == 1.0, table[1, k], jnp.where(
                        kind == 2.0, table[2, k], table[3, k]))) for k in range(3))
                exchange = STEP * exchange
                slope = (0.5 * STEP) * slope
                exchange_ref[z, part, rows, :] = exchange
                slope_ref[z, part, rows, :] = slope
                signed_ref[z, part, rows, :] = (
                    slope if part < 2 else -slope if part < 4 else jnp.where(upper_side, slope, -slope))
                axis_ref[z, part, rows, :] = (2.0 * STEP) * axis - 6.0 * exchange
        return carry

    lax.fori_loop(FIRST // 8, LAST // 8, body, 0)


def compute_kernel(index_ref, table, fields, end_ref, guess_ref,
                   state_even, state_odd, node_one, extra, rate_zero, rate_one, rate_two, node_two, sum_ref, difference_ref,
                   demag_ref, region, exchange_ref, slope_ref, signed_ref, axis_ref, sems):
    me = index_ref[0]
    aux = (exchange_ref, slope_ref, signed_ref, axis_ref, demag_ref, sum_ref, difference_ref)
    loads = [
        pltpu.make_async_copy(fields.at[6], region, sems.at[0]),
        pltpu.make_async_copy(fields.at[0:3], state_even, sems.at[1]),
        pltpu.make_async_copy(fields.at[3:6], demag_ref, sems.at[2]),
    ]
    for copy in loads:
        copy.start()
    loads[0].wait()
    fill_coefficients(table, region, exchange_ref, slope_ref, signed_ref, axis_ref)
    loads[1].wait()
    loads[2].wait()

    def load_start(target):
        copy = pltpu.make_async_copy(fields.at[0:3], target, sems.at[3])
        copy.start()
        copy.wait()

    def step_from(source, target, step):
        halo = me - step + DEPTH - 1

        @pl.when(step < me - 3)
        def _():
            def use(row, part, out, cells):
                for z in range(4):
                    put(target, (), z, part, row, [cells[c][z] + out[z][c] for c in range(3)])

            evaluate(source, aux, halo, use)

        @pl.when(step >= me - 3)
        def _():
            kept = step - me + 3

            def use(row, part, out, cells):
                for z in range(4):
                    put(target, (), z, part, row, [cells[c][z] + out[z][c] for c in range(3)])
                    put(rate_zero, (kept,), z, part, row, out[z])
                    put(node_one, (kept,), z, part, row, [cells[c][z] + 0.5 * out[z][c] for c in range(3)])

            evaluate(source, aux, halo, use)

    def advance(step, carry):
        even = lax.rem(step, 2) == 0
        pl.when(even)(lambda: step_from(state_even, state_odd, step))
        pl.when(jnp.logical_not(even))(lambda: step_from(state_odd, state_even, step))
        return carry

    lax.fori_loop(0, me + 1, advance, 0)
    pl.when(lax.rem(me, 2) == 0)(lambda: assemble(state_even, guess_ref))
    pl.when(lax.rem(me, 2) == 1)(lambda: assemble(state_odd, guess_ref))

    def sweep_slices(sweep, carry):
        halo = DEPTH - 2 - 2 * sweep

        def one_slice(count, carry):
            kept = 3 - count

            @pl.when((me - count >= 0) & (sweep == 0))
            def _():
                def use(row, part, out, cells):
                    for z in range(4):
                        put(node_two, (), z, part, row, [cells[c][z] + 0.5 * out[z][c] for c in range(3)])
                        put(rate_one, (kept,), z, part, row, out[z])

                evaluate(node_one.at[kept], aux, halo, use)

            @pl.when((me - count >= 0) & (sweep > 0))
            def _():
                def use(row, part, out, cells):
                    for z in range(4):
                        add = get(extra, (kept - 1,), z, part, row)
                        put(node_two, (), z, part, row, [cells[c][z] + 0.5 * out[z][c] + add[c] for c in range(3)])
                        put(rate_one, (kept,), z, part, row, out[z])

                evaluate(node_one.at[kept], aux, halo, use)

            pl.when((me - count == -1) & (sweep + 1 < ITERS))(lambda: load_start(node_two))

            @pl.when((count == 0) & (sweep + 1 < ITERS))
            def _():
                def use(row, part, out, cells):
                    for z in range(4):
                        put(rate_two, (), z, part, row, out[z])

                evaluate(node_two, aux, halo - 1, use)

            @pl.when((count > 0) & (me - count >= -1) & (sweep + 1 < ITERS))
            def _():
                def use(row, part, out, cells):
                    for z in range(4):
                        old = get(rate_zero, (kept + 1,), z, part, row)
                        mid = get(rate_one, (kept + 1,), z, part, row)
                        far = get(rate_two, (), z, part, row)
                        put(node_one, (kept + 1,), z, part, row, [
                            cells[c][z] + 0.5 * out[z][c] + (1.0 / 24.0) * (8.0 * mid[c] - 7.0 * old[c] - far[c])
                            for c in range(3)])
                        put(extra, (kept,), z, part, row, [
                            (1.0 / 24.0) * ((far[c] - old[c]) + 4.0 * (far[c] - mid[c]))
                            for c in range(3)])
                        put(rate_zero, (kept + 1,), z, part, row, out[z])
                        put(rate_two, (), z, part, row, out[z])

                evaluate(node_two, aux, halo - 1, use)

            return carry

        return lax.fori_loop(0, ITERS - sweep, one_slice, carry)

    lax.fori_loop(0, ITERS, sweep_slices, 0)
    assemble(node_two, end_ref)


def compute(index, table, fields, interpret=False):
    field = (3, 4, PARTS, ROWS, 128)
    vmem = pl.BlockSpec(memory_space=pltpu.VMEM)
    smem = pl.BlockSpec(memory_space=pltpu.SMEM)
    return pl.pallas_call(
        compute_kernel,
        name="llg",
        out_shape=[jax.ShapeDtypeStruct((3, 4, 64, 256), jnp.float32)] * 2,
        in_specs=[smem, smem, pl.BlockSpec(memory_space=pl.ANY)],
        out_specs=[vmem] * 2,
        scratch_shapes=[
            pltpu.VMEM(field, jnp.float32),
            pltpu.VMEM(field, jnp.float32),
            pltpu.VMEM((4,) + field, jnp.float32),
            pltpu.VMEM((3,) + field, jnp.float32),
            pltpu.VMEM((4,) + field, jnp.float32),
            pltpu.VMEM((4,) + field, jnp.float32),
            pltpu.VMEM(field, jnp.float32),
            pltpu.VMEM(field, jnp.float32),
            pltpu.VMEM(field, jnp.float32),
            pltpu.VMEM((2,) + field[1:], jnp.float32),
            pltpu.VMEM(field, jnp.float32),
        ] + [pltpu.VMEM(field[1:], jnp.float32)] * 5 + [pltpu.SemaphoreType.DMA((4,))],
        compiler_params=pltpu.CompilerParams(vmem_limit_bytes=62 * 1024 * 1024),
        interpret=interpret,
    )(index, table, fields)


def halo_kernel(start_ref, demag_ref, region_ref, out_ref, own, down, up, side_out, side_in, corner_out, corner_in, corner,
                send_sems, recv_sems, local_sems):
    gx, gy, tm = lax.axis_index("gx"), lax.axis_index("gy"), lax.axis_index("tm")
    count = lax.axis_size("gx")
    after = {"gx": lax.rem(gx + 1, count)}
    before = {"gx": lax.rem(gx + count - 1, count)}
    across = {"tm": tm + 1 - 2 * lax.rem(tm, 2), "gy": 1 - gy}
    barrier = pltpu.get_barrier_semaphore()
    for device in (after, before, across):
        pl.semaphore_signal(barrier, inc=1, device_id=device, device_id_type=MESH)

    upside_down = 7 - lax.broadcasted_iota(jnp.int32, (8, 128), 0)
    lane = lanes()

    def flip(value):
        return jnp.take_along_axis(value, upside_down, axis=0)

    def load(f, z, row, part):
        at = (z, slice(row, row + 8), slice(128 * part, 128 * part + 128))
        if f < 3:
            return start_ref[(f,) + at]
        if f < 6:
            return STEP * demag_ref[(f - 3,) + at]
        return region_ref[at].astype(jnp.float32)

    def quarters(a, b, c, d):
        return jnp.where(lane < 64, jnp.where(lane < 32, a, b), jnp.where(lane < 96, c, d))

    def stage(z, carry):
        for f in range(7):
            for k in range(4):
                rows = slice(8 * k, 8 * k + 8)
                a = [load(f, z, 8 * k, part) for part in range(2)]
                b = [flip(load(f, z, 56 - 8 * k, part)) for part in range(2)]
                for part in range(2):
                    own[f, z, part, rows, :] = a[part]
                    own[f, z, part + 2, rows, :] = b[part]
                side_out[f, z, rows, :] = quarters(a[0], pltpu.roll(b[0], 32, 1), pltpu.roll(b[1], 96, 1), a[1])
            for k in range(3):
                rows = slice(8 * k, 8 * k + 8)
                for part in range(2):
                    down[f, z, part, rows, :] = load(f, z, 40 + 8 * k, part)
                    up[f, z, part, rows, :] = flip(load(f, z, 16 - 8 * k, part))
        return carry

    lax.fori_loop(0, 4, stage, 0)
    pl.semaphore_wait(barrier, 3)

    def send(number, source, target, device):
        copy = pltpu.make_async_remote_copy(source, target, send_sems.at[number], recv_sems.at[number],
                                            device_id=device, device_id_type=MESH)
        copy.start()
        return copy

    near, far = slice(0, HALO), slice(HALO, 32)
    sides = [send(k, side_out.at[:, :, rows, :], side_in.at[:, :, rows, :], across) for k, rows in enumerate((near, far))]
    edge, inner = slice(FIRST, FIRST + HALO), slice(FIRST + HALO, LAST)
    edges = [send(2, down, out_ref.at[:, :, 0:2, edge, :], after), send(3, up, out_ref.at[:, :, 2:4, edge, :], before)]
    middle = pltpu.make_async_copy(own, out_ref.at[:, :, 0:4, inner, :], local_sems.at[0])
    middle.start()
    sides[0].wait_recv()

    def turn(pair, carry):
        for f in range(7):
            for k in range(3):
                rows = slice(8 * k, 8 * k + 8)
                back = slice(16 - 8 * k, 24 - 8 * k)
                one = flip(side_in[f, pair, back, :])
                two = flip(side_in[f, pair + 2, back, :])
                one_left, one_right = pltpu.roll(one, 96, 1), pltpu.roll(one, 32, 1)
                two_left, two_right = pltpu.roll(two, 96, 1), pltpu.roll(two, 32, 1)
                corner_out[0, f, pair, rows, :] = quarters(one_left, two_left, two_right, one_right)
                corner_out[1, f, pair, rows, :] = quarters(two_right, one_right, one_left, two_left)
        return carry

    lax.fori_loop(0, 2, turn, 0)
    corners = [send(4, corner_out.at[0], corner_in.at[0], after), send(5, corner_out.at[1], corner_in.at[1], before)]
    sides[1].wait_recv()
    strip = pltpu.make_async_copy(side_in, out_ref.at[:, :, 4, inner, :], local_sems.at[1])
    strip.start()
    corners[0].wait_recv()
    corners[1].wait_recv()
    mid = (lane >= 32) & (lane < 96)

    def unpack(pair, carry):
        for f in range(7):
            for k in range(3):
                rows = slice(8 * k, 8 * k + 8)
                upper, lower = corner_in[0, f, pair, rows, :], corner_in[1, f, pair, rows, :]
                corner[f, pair, rows, :] = jnp.where(mid, lower, upper)
                corner[f, pair + 2, rows, :] = pltpu.roll(jnp.where(mid, upper, lower), 64, 1)
        return carry

    lax.fori_loop(0, 2, unpack, 0)
    last = pltpu.make_async_copy(corner, out_ref.at[:, :, 4, edge, :], local_sems.at[2])
    last.start()
    for copy in edges:
        copy.wait()
    for copy in sides + corners:
        copy.wait_send()
    middle.wait()
    strip.wait()
    last.wait()


def gather_halo(start_field, demag_field, region_map):
    vmem = pl.BlockSpec(memory_space=pltpu.VMEM)
    return pl.pallas_call(
        halo_kernel,
        name="halo",
        out_shape=jax.ShapeDtypeStruct((7, 4, PARTS, ROWS, 128), jnp.float32),
        in_specs=[vmem] * 3,
        out_specs=pl.BlockSpec(memory_space=pl.ANY),
        scratch_shapes=[
            pltpu.VMEM((7, 4, 4, 32, 128), jnp.float32),
            pltpu.VMEM((7, 4, 2, HALO, 128), jnp.float32),
            pltpu.VMEM((7, 4, 2, HALO, 128), jnp.float32),
            pltpu.VMEM((7, 4, 32, 128), jnp.float32),
            pltpu.VMEM((7, 4, 32, 128), jnp.float32),
            pltpu.VMEM((2, 7, 2, HALO, 128), jnp.float32),
            pltpu.VMEM((2, 7, 2, HALO, 128), jnp.float32),
            pltpu.VMEM((7, 4, HALO, 128), jnp.float32),
            pltpu.SemaphoreType.DMA((6,)),
            pltpu.SemaphoreType.DMA((6,)),
            pltpu.SemaphoreType.DMA((3,)),
        ],
        compiler_params=pltpu.CompilerParams(
            collective_id=0, has_side_effects=True, vmem_limit_bytes=40 * 1024 * 1024),
    )(start_field, demag_field, region_map)


def on_device(start_field, demag_field, region_map, material_table):
    fields = gather_halo(start_field, demag_field, region_map)
    index = lax.axis_index("tm").astype(jnp.int32)[None]
    end, guess = compute(index, material_table, fields)
    return end[None], guess[None]


def solution(mesh):
    placed = (P(None, None, "gx", "gy"), P(None, None, "gx", "gy"), P(None, "gx", "gy"), P())
    return jax.shard_map(
        on_device,
        mesh=mesh,
        in_specs=placed,
        out_specs=(P("tm", None, None, "gx", "gy"), P("tm", None, None, "gx", "gy")),
        check_vma=False,
    )
```

```python
import jax
import jax.numpy as jnp
from jax import lax
from jax.experimental import pallas as pl
from jax.experimental.pallas import tpu as pltpu
from jax.sharding import PartitionSpec as P

MESH = pl.DeviceIdType.MESH
ITERS = 4
HALO = 24
SIDE = 32
STEP = 0.05
DEPTH = 8
FIRST = 8
LAST = 64
ROWS = 72
PARTS = 5


def blocks_of(halo):
    return (FIRST + HALO - halo) // 8, LAST // 8


def lanes():
    return lax.broadcasted_iota(jnp.int32, (8, 128), 1)


def neighbours(field, c, z, row):
    rows = pl.ds(row, 8)
    lane = lanes()
    first, last = lane == 0, lane == 127
    v = [field[c, z, part, rows, :] for part in range(PARTS)]
    n0, n2, n4 = (pltpu.roll(v[part], 127, 1) for part in (0, 2, 4))
    p1, p3, p4 = (pltpu.roll(v[part], 1, 1) for part in (1, 3, 4))
    ahead = pltpu.roll(jnp.where(lane == 32, v[4], v[2]), 95, 1)
    behind = pltpu.roll(jnp.where(lane == 95, v[4], v[3]), 33, 1)
    following = [
        v[1],
        jnp.where(last, n4, n0),
        v[3],
        jnp.where(last, ahead, n2),
        jnp.where(last, n0, jnp.where(lane == 95, ahead, n4)),
    ]
    previous = [
        jnp.where(first, p4, p1),
        v[0],
        jnp.where(first, behind, p3),
        v[2],
        jnp.where(first, p1, jnp.where(lane == 32, behind, p4)),
    ]
    return following, previous


def join_halves(field):
    lane = lax.broadcasted_iota(jnp.int32, (1, 128), 1)
    down = (lane < 32) | ((lane >= 64) & (lane < 96))
    edge, beyond = pl.ds(LAST - 1, 1), pl.ds(LAST, 1)
    for c in range(3):
        for z in range(4):
            for part in range(4):
                field[c, z, part, beyond, :] = field[c, z, (part + 2) % 4, edge, :]
            side = field[c, z, 4, edge, :]
            field[c, z, 4, beyond, :] = jnp.where(down, pltpu.roll(side, 96, 1), pltpu.roll(side, 32, 1))


def rates(field, aux, row, part, z, following, previous):
    exchange_ref, slope_ref, signed_ref, axis_ref, demag_ref = aux
    rows = pl.ds(row, 8)
    above = pl.ds(row - 1, 8)
    below = pl.ds(row + 1, 8)
    sums = []
    slope_x = [None] * 3
    center = [field[c, z, part, rows, :] for c in range(3)]
    for c in range(3):
        x_next = field[c, z, part, below, :]
        x_prev = field[c, z, part, above, :]
        if z in (0, 3):
            z_pair = field[c, 1 if z == 0 else 2, part, rows, :]
        else:
            z_pair = field[c, z + 1, part, rows, :] + field[c, z - 1, part, rows, :]
        sums.append((x_next + x_prev) + (following[c][part] + previous[c][part]) + z_pair)
        if c != 1:
            slope_x[c] = x_next - x_prev
    mx, my, mz = center
    own = 5.0 if z in (0, 3) else 6.0
    exchange = exchange_ref[z, part, rows, :]
    slope = slope_ref[z, part, rows, :]
    signed = signed_ref[z, part, rows, :]
    axis = axis_ref[z, part, rows, :]
    hx = exchange * (sums[0] - own * mx) + signed * slope_x[2] + demag_ref[0, z, part, rows, :]
    hy = (exchange * (sums[1] - own * my) + slope * (following[2][part] - previous[2][part])
          + demag_ref[1, z, part, rows, :])
    hz = (exchange * sums[2] + axis * mz
          - (signed * slope_x[0] + slope * (following[1][part] - previous[1][part])) + demag_ref[2, z, part, rows, :])
    gx = hx + (my * hz - mz * hy)
    gy = hy + (mz * hx - mx * hz)
    gz = hz + (mx * hy - my * hx)
    return (gy * mz - gz * my, gz * mx - gx * mz, gx * my - gy * mx), center


def put(ref, lead, z, part, row, values):
    for c in range(3):
        ref[(*lead, c, z, part, pl.ds(row, 8), slice(None))] = values[c]


def get(ref, lead, z, part, row):
    return [ref[(*lead, c, z, part, pl.ds(row, 8), slice(None))] for c in range(3)]


def evaluate(field, aux, halo, use):
    first, last = blocks_of(halo)
    join_halves(field)

    def run(block, carry):
        row = pl.multiple_of(block * 8, 8)
        for z in range(4):
            both = [neighbours(field, c, z, row) for c in range(3)]
            following, previous = [pair[0] for pair in both], [pair[1] for pair in both]
            for part in range(PARTS):
                out, cells = rates(field, aux, row, part, z, following, previous)
                use(row, part, z, out, cells)
        return carry

    pairs = (last - first) // 2

    def two(pair, carry):
        return run(first + 2 * pair + 1, run(first + 2 * pair, carry))

    lax.fori_loop(0, pairs, two, 0)
    lax.fori_loop(first + 2 * pairs, last, run, 0)


def permuted(values, permutation):
    high = values.astype(jnp.bfloat16)
    rest = values - high.astype(jnp.float32)
    middle = rest.astype(jnp.bfloat16)
    low = (rest - middle.astype(jnp.float32)).astype(jnp.bfloat16)
    product = jnp.dot(jnp.concatenate([high, middle, low], axis=0), permutation, preferred_element_type=jnp.float32)
    count = values.shape[0]
    return (product[:count] + product[count:2 * count]) + product[2 * count:]


def spread(natural_axis):
    natural = lax.broadcasted_iota(jnp.int32, (256, 256), natural_axis)
    sorted_at = lax.broadcasted_iota(jnp.int32, (256, 256), 1 - natural_axis)
    source = jnp.where(sorted_at < 128, 2 * sorted_at, 2 * sorted_at - 255)
    return (natural == source).astype(jnp.float32).astype(jnp.bfloat16)


def assemble(field, out_ref, order_ref):
    upside_down = 7 - lax.broadcasted_iota(jnp.int32, (8, 128), 0)
    inner = pl.ds(FIRST + HALO, 32)

    def body(z, carry):
        for c in range(3):
            sorted_rows = jnp.concatenate(
                [jnp.concatenate([field[c, z, part, inner, :], field[c, z, part + 1, inner, :]], axis=1) for part in (0, 2)],
                axis=0)
            rows = 2.0 * permuted(sorted_rows, order_ref[...])
            out_ref[c, z, 0:32, :] = rows[:32]
            for block in range(4):
                for columns in (slice(0, 128), slice(128, 256)):
                    out_ref[c, z, 32 + 8 * block:40 + 8 * block, columns] = jnp.take_along_axis(
                        rows[56 - 8 * block:64 - 8 * block, columns], upside_down, axis=0)
        return carry

    lax.fori_loop(0, 4, body, 0)


def fill_coefficients(table, region, exchange_ref, slope_ref, signed_ref, axis_ref):
    lane = lanes()
    upper_side = (lane < 32) | (lane >= 96)

    def body(block, carry):
        rows = pl.ds(pl.multiple_of(block * 8, 8), 8)
        for z in range(4):
            for part in range(PARTS):
                kind = region[z, part, rows, :]
                exchange, slope, axis = (
                    jnp.where(kind == 0.0, table[0, k], jnp.where(kind == 1.0, table[1, k], jnp.where(
                        kind == 2.0, table[2, k], table[3, k]))) for k in range(3))
                exchange = (2.0 * STEP) * exchange
                slope = STEP * slope
                exchange_ref[z, part, rows, :] = exchange
                slope_ref[z, part, rows, :] = slope
                signed_ref[z, part, rows, :] = (
                    slope if part < 2 else -slope if part < 4 else jnp.where(upper_side, slope, -slope))
                axis_ref[z, part, rows, :] = (4.0 * STEP) * axis - (5.0 if z in (0, 3) else 6.0) * exchange
        return carry

    lax.fori_loop(FIRST // 8, LAST // 8, body, 0)


def halve(refs):
    def body(block, carry):
        rows = pl.ds(pl.multiple_of(block * 8, 8), 8)
        for ref in refs:
            for z in range(4):
                for part in range(PARTS):
                    for lead in ((),) if len(ref.shape) == 4 else ((0,), (1,), (2,)):
                        at = (*lead, z, part, rows, slice(None))
                        ref[at] = 0.5 * ref[at]
        return carry

    lax.fori_loop(blocks_of(DEPTH - 1)[0], LAST // 8, body, 0)


def compute_kernel(index_ref, table, fields, end_ref, guess_ref,
                   state_even, state_odd, node_one, extra, rate_zero, rate_one, rate_two, node_two,
                   demag_ref, region, exchange_ref, slope_ref, signed_ref, axis_ref, order_ref, sems):
    me = index_ref[0]
    aux = (exchange_ref, slope_ref, signed_ref, axis_ref, demag_ref)
    loads = [
        pltpu.make_async_copy(fields.at[6], region, sems.at[0]),
        pltpu.make_async_copy(fields.at[0:3], state_even, sems.at[1]),
        pltpu.make_async_copy(fields.at[3:6], demag_ref, sems.at[2]),
    ]
    for copy in loads:
        copy.start()
    order_ref[...] = spread(1)
    loads[0].wait()
    fill_coefficients(table, region, exchange_ref, slope_ref, signed_ref, axis_ref)
    loads[1].wait()
    loads[2].wait()

    def load_start(target):
        copy = pltpu.make_async_copy(fields.at[0:3], target, sems.at[3])
        copy.start()
        copy.wait()

    def step_from(source, target, step):
        halo = me - step + DEPTH - 1

        @pl.when(step < me - 3)
        def _():
            def use(row, part, z, out, cells):
                put(target, (), z, part, row, [cells[c] + out[c] for c in range(3)])

            evaluate(source, aux, halo, use)

        @pl.when(step >= me - 3)
        def _():
            kept = step - me + 3

            def use(row, part, z, out, cells):
                half = [0.5 * out[c] for c in range(3)]
                put(target, (), z, part, row, [cells[c] + out[c] for c in range(3)])
                put(rate_zero, (kept,), z, part, row, half)
                put(node_one, (kept,), z, part, row, [cells[c] + half[c] for c in range(3)])

            evaluate(source, aux, halo, use)

    def advance(step, carry):
        even = lax.rem(step, 2) == 0
        pl.when(even)(lambda: step_from(state_even, state_odd, step))
        pl.when(jnp.logical_not(even))(lambda: step_from(state_odd, state_even, step))
        return carry

    lax.fori_loop(0, me + 1, advance, 0)
    halve(aux)
    pl.when(lax.rem(me, 2) == 0)(lambda: assemble(state_even, guess_ref, order_ref))
    pl.when(lax.rem(me, 2) == 1)(lambda: assemble(state_odd, guess_ref, order_ref))

    def sweep_slices(sweep, carry):
        halo = DEPTH - 2 - 2 * sweep

        def one_slice(count, carry):
            kept = 3 - count

            @pl.when((me - count >= 0) & (sweep == 0))
            def _():
                def use(row, part, z, out, cells):
                    put(node_two, (), z, part, row, [cells[c] + out[c] for c in range(3)])
                    put(rate_one, (kept,), z, part, row, out)

                evaluate(node_one.at[kept], aux, halo, use)

            @pl.when((me - count >= 0) & (sweep > 0))
            def _():
                def use(row, part, z, out, cells):
                    add = get(extra, (kept - 1,), z, part, row)
                    put(node_two, (), z, part, row, [cells[c] + out[c] + add[c] for c in range(3)])
                    put(rate_one, (kept,), z, part, row, out)

                evaluate(node_one.at[kept], aux, halo, use)

            pl.when((me - count == -1) & (sweep + 1 < ITERS))(lambda: load_start(node_two))

            @pl.when((count == 0) & (sweep + 1 < ITERS))
            def _():
                def use(row, part, z, out, cells):
                    put(rate_two, (), z, part, row, out)

                evaluate(node_two, aux, halo - 1, use)

            @pl.when((count > 0) & (me - count >= -1) & (sweep + 1 < ITERS))
            def _():
                def use(row, part, z, out, cells):
                    old = get(rate_zero, (kept + 1,), z, part, row)
                    mid = get(rate_one, (kept + 1,), z, part, row)
                    far = get(rate_two, (), z, part, row)
                    put(node_one, (kept + 1,), z, part, row, [
                        cells[c] + out[c] + (1.0 / 12.0) * (8.0 * mid[c] - 7.0 * old[c] - far[c])
                        for c in range(3)])
                    put(extra, (kept,), z, part, row, [
                        (1.0 / 12.0) * ((far[c] - old[c]) + 4.0 * (far[c] - mid[c]))
                        for c in range(3)])
                    put(rate_zero, (kept + 1,), z, part, row, out)
                    put(rate_two, (), z, part, row, out)

                evaluate(node_two, aux, halo - 1, use)

            return carry

        return lax.fori_loop(0, ITERS - sweep, one_slice, carry)

    lax.fori_loop(0, ITERS, sweep_slices, 0)
    assemble(node_two, end_ref, order_ref)


def compute(index, table, fields, interpret=False):
    field = (3, 4, PARTS, ROWS, 128)
    vmem = pl.BlockSpec(memory_space=pltpu.VMEM)
    smem = pl.BlockSpec(memory_space=pltpu.SMEM)
    return pl.pallas_call(
        compute_kernel,
        name="llg",
        out_shape=[jax.ShapeDtypeStruct((3, 4, 64, 256), jnp.float32)] * 2,
        in_specs=[smem, smem, pl.BlockSpec(memory_space=pltpu.HBM)],
        out_specs=[vmem] * 2,
        scratch_shapes=[
            pltpu.VMEM(field, jnp.float32),
            pltpu.VMEM(field, jnp.float32),
            pltpu.VMEM((4,) + field, jnp.float32),
            pltpu.VMEM((3,) + field, jnp.float32),
            pltpu.VMEM((4,) + field, jnp.float32),
            pltpu.VMEM((4,) + field, jnp.float32),
            pltpu.VMEM(field, jnp.float32),
            pltpu.VMEM(field, jnp.float32),
            pltpu.VMEM(field, jnp.float32),
        ] + [pltpu.VMEM(field[1:], jnp.float32)] * 5 + [
            pltpu.VMEM((256, 256), jnp.bfloat16), pltpu.SemaphoreType.DMA((4,))],
        compiler_params=pltpu.CompilerParams(vmem_limit_bytes=62 * 1024 * 1024),
        interpret=interpret,
    )(index, table, fields)


def halo_kernel(start_hbm, demag_hbm, region_hbm, out_ref, start_ref, demag_ref, region_ref, order_ref, own, down, up, side_out, side_in, corner_out, corner_in, corner,
                send_sems, recv_sems, local_sems):
    gx, gy, tm = lax.axis_index("gx"), lax.axis_index("gy"), lax.axis_index("tm")
    count = lax.axis_size("gx")
    after = {"gx": lax.rem(gx + 1, count)}
    before = {"gx": lax.rem(gx + count - 1, count)}
    across = {"tm": tm + 1 - 2 * lax.rem(tm, 2), "gy": 1 - gy}
    loads = [pltpu.make_async_copy(source, target, local_sems.at[3 + k]) for k, (source, target) in enumerate(
        ((start_hbm, start_ref), (demag_hbm, demag_ref), (region_hbm, region_ref)))]
    for copy in loads:
        copy.start()
    barrier = pltpu.get_barrier_semaphore()
    for device in (after, before, across):
        pl.semaphore_signal(barrier, inc=1, device_id=device, device_id_type=MESH)

    upside_down = 7 - lax.broadcasted_iota(jnp.int32, (8, 128), 0)
    lane = lanes()

    def flip(value):
        return jnp.take_along_axis(value, upside_down, axis=0)

    def load(f, z):
        if f < 3:
            return 0.5 * start_ref[f, z]
        if f < 6:
            return STEP * demag_ref[f - 3, z]
        return region_ref[z].astype(jnp.float32)

    def quarters(a, b, c, d):
        return jnp.where(lane < 64, jnp.where(lane < 32, a, b), jnp.where(lane < 96, c, d))

    def piece(values, row, part):
        return values[row:row + 8, 128 * part:128 * part + 128]

    def stage_sides(z, carry):
        for f in range(7):
            tile = load(f, z)
            for k in range(4):
                a = [piece(tile, 8 * k, part) for part in range(2)]
                b = [flip(piece(tile, 56 - 8 * k, part)) for part in range(2)]
                side_out[f, z, 8 * k:8 * k + 8, :] = quarters(a[0], pltpu.roll(b[0], 32, 1), pltpu.roll(b[1], 96, 1), a[1])
        return carry

    def stage_rows(z, carry):
        for f in range(7):
            tile = load(f, z)
            if f < 6:
                halves = permuted(tile, order_ref[...])
            else:
                halves = jnp.dot(tile.astype(jnp.bfloat16), order_ref[...], preferred_element_type=jnp.float32)
            for k in range(4):
                rows = slice(8 * k, 8 * k + 8)
                for part in range(2):
                    own[f, z, part, rows, :] = piece(halves, 8 * k, part)
                    own[f, z, part + 2, rows, :] = flip(piece(halves, 56 - 8 * k, part))
            for k in range(3):
                rows = slice(8 * k, 8 * k + 8)
                for part in range(2):
                    down[f, z, part, rows, :] = piece(halves, 40 + 8 * k, part)
                    up[f, z, part, rows, :] = flip(piece(halves, 16 - 8 * k, part))
        return carry

    def send(number, source, target, device):
        copy = pltpu.make_async_remote_copy(source, target, send_sems.at[number], recv_sems.at[number],
                                            device_id=device, device_id_type=MESH)
        copy.start()
        return copy

    for copy in loads:
        copy.wait()
    lax.fori_loop(0, 4, stage_sides, 0)
    pl.semaphore_wait(barrier, 3)
    near, far = slice(0, HALO), slice(HALO, 32)
    sides = [send(k, side_out.at[:, :, rows, :], side_in.at[:, :, rows, :], across) for k, rows in enumerate((near, far))]
    order_ref[...] = spread(0)
    lax.fori_loop(0, 4, stage_rows, 0)
    edge, inner = slice(FIRST, FIRST + HALO), slice(FIRST + HALO, LAST)
    edges = [send(2, down, out_ref.at[:, :, 0:2, edge, :], after), send(3, up, out_ref.at[:, :, 2:4, edge, :], before)]
    middle = pltpu.make_async_copy(own, out_ref.at[:, :, 0:4, inner, :], local_sems.at[0])
    middle.start()
    sides[0].wait_recv()

    def turn(pair, carry):
        for f in range(7):
            for k in range(3):
                rows = slice(8 * k, 8 * k + 8)
                back = slice(16 - 8 * k, 24 - 8 * k)
                one = flip(side_in[f, pair, back, :])
                two = flip(side_in[f, pair + 2, back, :])
                one_left, one_right = pltpu.roll(one, 96, 1), pltpu.roll(one, 32, 1)
                two_left, two_right = pltpu.roll(two, 96, 1), pltpu.roll(two, 32, 1)
                corner_out[0, f, pair, rows, :] = quarters(one_left, two_left, two_right, one_right)
                corner_out[1, f, pair, rows, :] = quarters(two_right, one_right, one_left, two_left)
        return carry

    lax.fori_loop(0, 2, turn, 0)
    corners = [send(4, corner_out.at[0], corner_in.at[0], after), send(5, corner_out.at[1], corner_in.at[1], before)]
    sides[1].wait_recv()
    strip = pltpu.make_async_copy(side_in, out_ref.at[:, :, 4, inner, :], local_sems.at[1])
    strip.start()
    corners[0].wait_recv()
    corners[1].wait_recv()
    mid = (lane >= 32) & (lane < 96)

    def unpack(pair, carry):
        for f in range(7):
            for k in range(3):
                rows = slice(8 * k, 8 * k + 8)
                upper, lower = corner_in[0, f, pair, rows, :], corner_in[1, f, pair, rows, :]
                corner[f, pair, rows, :] = jnp.where(mid, lower, upper)
                corner[f, pair + 2, rows, :] = pltpu.roll(jnp.where(mid, upper, lower), 64, 1)
        return carry

    lax.fori_loop(0, 2, unpack, 0)
    last = pltpu.make_async_copy(corner, out_ref.at[:, :, 4, edge, :], local_sems.at[2])
    last.start()
    for copy in edges:
        copy.wait()
    for copy in sides + corners:
        copy.wait_send()
    middle.wait()
    strip.wait()
    last.wait()


def gather_halo(start_field, demag_field, region_map):
    hbm = pl.BlockSpec(memory_space=pltpu.HBM)
    return pl.pallas_call(
        halo_kernel,
        name="halo",
        out_shape=jax.ShapeDtypeStruct((7, 4, PARTS, ROWS, 128), jnp.float32),
        in_specs=[hbm] * 3,
        out_specs=hbm,
        scratch_shapes=[
            pltpu.VMEM((3, 4, 64, 256), jnp.float32),
            pltpu.VMEM((3, 4, 64, 256), jnp.float32),
            pltpu.VMEM((4, 64, 256), jnp.int32),
            pltpu.VMEM((256, 256), jnp.bfloat16),
            pltpu.VMEM((7, 4, 4, 32, 128), jnp.float32),
            pltpu.VMEM((7, 4, 2, HALO, 128), jnp.float32),
            pltpu.VMEM((7, 4, 2, HALO, 128), jnp.float32),
            pltpu.VMEM((7, 4, 32, 128), jnp.float32),
            pltpu.VMEM((7, 4, 32, 128), jnp.float32),
            pltpu.VMEM((2, 7, 2, HALO, 128), jnp.float32),
            pltpu.VMEM((2, 7, 2, HALO, 128), jnp.float32),
            pltpu.VMEM((7, 4, HALO, 128), jnp.float32),
            pltpu.SemaphoreType.DMA((6,)),
            pltpu.SemaphoreType.DMA((6,)),
            pltpu.SemaphoreType.DMA((6,)),
        ],
        compiler_params=pltpu.CompilerParams(
            collective_id=0, has_side_effects=True, vmem_limit_bytes=62 * 1024 * 1024),
    )(start_field, demag_field, region_map)


def on_device(start_field, demag_field, region_map, material_table):
    fields = gather_halo(start_field, demag_field, region_map)
    index = lax.axis_index("tm").astype(jnp.int32)[None]
    end, guess = compute(index, material_table, fields)
    return end[None], guess[None]


def solution(mesh):
    placed = (P(None, None, "gx", "gy"), P(None, None, "gx", "gy"), P(None, "gx", "gy"), P())
    return jax.shard_map(
        on_device,
        mesh=mesh,
        in_specs=placed,
        out_specs=(P("tm", None, None, "gx", "gy"), P("tm", None, None, "gx", "gy")),
        check_vma=False,
    )
```

```python
import jax
import jax.numpy as jnp
from jax import lax
from jax.experimental import pallas as pl
from jax.experimental.pallas import tpu as pltpu
from jax.sharding import PartitionSpec as P

MESH = pl.DeviceIdType.MESH
ITERS = 4
HALO = 24
SIDE = 32
STEP = 0.05
DEPTH = 8
FIRST = 8
LAST = 64
ROWS = 72
PARTS = 5


def blocks_of(halo):
    return (FIRST + HALO - halo) // 8, LAST // 8


def lanes():
    return lax.broadcasted_iota(jnp.int32, (8, 128), 1)


def neighbours(field, c, z, row):
    rows = pl.ds(row, 8)
    lane = lanes()
    first, last = lane == 0, lane == 127
    v = [field[c, z, part, rows, :] for part in range(PARTS)]
    n0, n2, n4 = (pltpu.roll(v[part], 127, 1) for part in (0, 2, 4))
    p1, p3, p4 = (pltpu.roll(v[part], 1, 1) for part in (1, 3, 4))
    ahead = pltpu.roll(jnp.where(lane == 32, v[4], v[2]), 95, 1)
    behind = pltpu.roll(jnp.where(lane == 95, v[4], v[3]), 33, 1)
    following = [
        v[1],
        jnp.where(last, n4, n0),
        v[3],
        jnp.where(last, ahead, n2),
        jnp.where(last, n0, jnp.where(lane == 95, ahead, n4)),
    ]
    previous = [
        jnp.where(first, p4, p1),
        v[0],
        jnp.where(first, behind, p3),
        v[2],
        jnp.where(first, p1, jnp.where(lane == 32, behind, p4)),
    ]
    return following, previous


def join_halves(field):
    lane = lax.broadcasted_iota(jnp.int32, (1, 128), 1)
    down = (lane < 32) | ((lane >= 64) & (lane < 96))
    edge, beyond = pl.ds(LAST - 1, 1), pl.ds(LAST, 1)
    for c in range(3):
        for z in range(4):
            for part in range(4):
                field[c, z, part, beyond, :] = field[c, z, (part + 2) % 4, edge, :]
            side = field[c, z, 4, edge, :]
            field[c, z, 4, beyond, :] = jnp.where(down, pltpu.roll(side, 96, 1), pltpu.roll(side, 32, 1))


def rates(field, aux, row, part, z, following, previous):
    exchange_ref, slope_ref, signed_ref, axis_ref, demag_ref = aux
    rows = pl.ds(row, 8)
    above = pl.ds(row - 1, 8)
    below = pl.ds(row + 1, 8)
    sums = []
    slope_x = [None] * 3
    center = [field[c, z, part, rows, :] for c in range(3)]
    for c in range(3):
        x_next = field[c, z, part, below, :]
        x_prev = field[c, z, part, above, :]
        if z in (0, 3):
            z_pair = field[c, 1 if z == 0 else 2, part, rows, :]
        else:
            z_pair = field[c, z + 1, part, rows, :] + field[c, z - 1, part, rows, :]
        sums.append((x_next + x_prev) + (following[c][part] + previous[c][part]) + z_pair)
        if c != 1:
            slope_x[c] = x_next - x_prev
    mx, my, mz = center
    own = 5.0 if z in (0, 3) else 6.0
    exchange = exchange_ref[z, part, rows, :]
    slope = slope_ref[z, part, rows, :]
    signed = signed_ref[z, part, rows, :]
    axis = axis_ref[z, part, rows, :]
    hx = exchange * (sums[0] - own * mx) + signed * slope_x[2] + demag_ref[0, z, part, rows, :]
    hy = (exchange * (sums[1] - own * my) + slope * (following[2][part] - previous[2][part])
          + demag_ref[1, z, part, rows, :])
    hz = (exchange * sums[2] + axis * mz
          - (signed * slope_x[0] + slope * (following[1][part] - previous[1][part])) + demag_ref[2, z, part, rows, :])
    gx = hx + (my * hz - mz * hy)
    gy = hy + (mz * hx - mx * hz)
    gz = hz + (mx * hy - my * hx)
    return (gy * mz - gz * my, gz * mx - gx * mz, gx * my - gy * mx), center


def put(ref, lead, z, part, row, values):
    for c in range(3):
        ref[(*lead, c, z, part, pl.ds(row, 8), slice(None))] = values[c]


def get(ref, lead, z, part, row):
    return [ref[(*lead, c, z, part, pl.ds(row, 8), slice(None))] for c in range(3)]


def evaluate(field, aux, halo, use):
    first, last = blocks_of(halo)
    join_halves(field)

    def run(block, carry):
        row = pl.multiple_of(block * 8, 8)
        for z in range(4):
            both = [neighbours(field, c, z, row) for c in range(3)]
            following, previous = [pair[0] for pair in both], [pair[1] for pair in both]
            for part in range(PARTS):
                out, cells = rates(field, aux, row, part, z, following, previous)
                use(row, part, z, out, cells)
        return carry

    pairs = (last - first) // 2

    def two(pair, carry):
        return run(first + 2 * pair + 1, run(first + 2 * pair, carry))

    lax.fori_loop(0, pairs, two, 0)
    lax.fori_loop(first + 2 * pairs, last, run, 0)


def permuted(values, permutation):
    high = values.astype(jnp.bfloat16)
    rest = values - high.astype(jnp.float32)
    middle = rest.astype(jnp.bfloat16)
    low = (rest - middle.astype(jnp.float32)).astype(jnp.bfloat16)
    product = jnp.dot(jnp.concatenate([high, middle, low], axis=0), permutation, preferred_element_type=jnp.float32)
    count = values.shape[0]
    return (product[:count] + product[count:2 * count]) + product[2 * count:]


def spread(natural_axis):
    natural = lax.broadcasted_iota(jnp.int32, (256, 256), natural_axis)
    sorted_at = lax.broadcasted_iota(jnp.int32, (256, 256), 1 - natural_axis)
    source = jnp.where(sorted_at < 128, 2 * sorted_at, 2 * sorted_at - 255)
    return (natural == source).astype(jnp.float32).astype(jnp.bfloat16)


def assemble(field, out_ref, out_hbm, sem, order_ref):
    upside_down = 7 - lax.broadcasted_iota(jnp.int32, (8, 128), 0)
    inner = pl.ds(FIRST + HALO, 32)

    def body(z, carry):
        for c in range(3):
            sorted_rows = jnp.concatenate(
                [jnp.concatenate([field[c, z, part, inner, :], field[c, z, part + 1, inner, :]], axis=1) for part in (0, 2)],
                axis=0)
            rows = 2.0 * permuted(sorted_rows, order_ref[...])
            out_ref[c, z, 0:32, :] = rows[:32]
            for block in range(4):
                for columns in (slice(0, 128), slice(128, 256)):
                    out_ref[c, z, 32 + 8 * block:40 + 8 * block, columns] = jnp.take_along_axis(
                        rows[56 - 8 * block:64 - 8 * block, columns], upside_down, axis=0)
        pltpu.make_async_copy(out_ref.at[:, z], out_hbm.at[:, z], sem).start()
        return carry

    lax.fori_loop(0, 4, body, 0)


def fill_coefficients(table, region, exchange_ref, slope_ref, signed_ref, axis_ref):
    lane = lanes()
    upper_side = (lane < 32) | (lane >= 96)

    def body(block, carry):
        rows = pl.ds(pl.multiple_of(block * 8, 8), 8)
        for z in range(4):
            for part in range(PARTS):
                kind = region[z, part, rows, :]
                exchange, slope, axis = (
                    jnp.where(kind == 0.0, table[0, k], jnp.where(kind == 1.0, table[1, k], jnp.where(
                        kind == 2.0, table[2, k], table[3, k]))) for k in range(3))
                exchange = (2.0 * STEP) * exchange
                slope = STEP * slope
                exchange_ref[z, part, rows, :] = exchange
                slope_ref[z, part, rows, :] = slope
                signed_ref[z, part, rows, :] = (
                    slope if part < 2 else -slope if part < 4 else jnp.where(upper_side, slope, -slope))
                axis_ref[z, part, rows, :] = (4.0 * STEP) * axis - (5.0 if z in (0, 3) else 6.0) * exchange
        return carry

    lax.fori_loop(FIRST // 8, LAST // 8, body, 0)


def halve(refs):
    def body(block, carry):
        rows = pl.ds(pl.multiple_of(block * 8, 8), 8)
        for ref in refs:
            for z in range(4):
                for part in range(PARTS):
                    for lead in ((),) if len(ref.shape) == 4 else ((0,), (1,), (2,)):
                        at = (*lead, z, part, rows, slice(None))
                        ref[at] = 0.5 * ref[at]
        return carry

    lax.fori_loop(blocks_of(DEPTH - 1)[0], LAST // 8, body, 0)


def compute_kernel(index_ref, table, fields, end_hbm, guess_hbm, end_ref, guess_ref,
                   state_even, state_odd, node_one, extra, rate_zero, rate_one, rate_two, node_two,
                   demag_ref, region, exchange_ref, slope_ref, signed_ref, axis_ref, order_ref, sems):
    me = index_ref[0]
    aux = (exchange_ref, slope_ref, signed_ref, axis_ref, demag_ref)
    loads = [
        pltpu.make_async_copy(fields.at[6], region, sems.at[0]),
        pltpu.make_async_copy(fields.at[0:3], state_even, sems.at[1]),
        pltpu.make_async_copy(fields.at[3:6], demag_ref, sems.at[2]),
    ]
    for copy in loads:
        copy.start()
    order_ref[...] = spread(1)
    loads[0].wait()
    fill_coefficients(table, region, exchange_ref, slope_ref, signed_ref, axis_ref)
    loads[1].wait()
    loads[2].wait()

    def load_start(target):
        copy = pltpu.make_async_copy(fields.at[0:3], target, sems.at[3])
        copy.start()
        copy.wait()

    def step_from(source, target, step):
        halo = me - step + DEPTH - 1

        @pl.when(step < me - 3)
        def _():
            def use(row, part, z, out, cells):
                put(target, (), z, part, row, [cells[c] + out[c] for c in range(3)])

            evaluate(source, aux, halo, use)

        @pl.when(step >= me - 3)
        def _():
            kept = step - me + 3

            def use(row, part, z, out, cells):
                half = [0.5 * out[c] for c in range(3)]
                put(target, (), z, part, row, [cells[c] + out[c] for c in range(3)])
                put(rate_zero, (kept,), z, part, row, half)
                put(node_one, (kept,), z, part, row, [cells[c] + half[c] for c in range(3)])

            evaluate(source, aux, halo, use)

    def advance(step, carry):
        even = lax.rem(step, 2) == 0
        pl.when(even)(lambda: step_from(state_even, state_odd, step))
        pl.when(jnp.logical_not(even))(lambda: step_from(state_odd, state_even, step))
        return carry

    lax.fori_loop(0, me + 1, advance, 0)
    halve(aux)
    pl.when(lax.rem(me, 2) == 0)(lambda: assemble(state_even, guess_ref, guess_hbm, sems.at[4], order_ref))
    pl.when(lax.rem(me, 2) == 1)(lambda: assemble(state_odd, guess_ref, guess_hbm, sems.at[4], order_ref))

    def sweep_slices(sweep, carry):
        halo = DEPTH - 2 - 2 * sweep

        def one_slice(count, carry):
            kept = 3 - count

            @pl.when((me - count >= 0) & (sweep == 0))
            def _():
                def use(row, part, z, out, cells):
                    put(node_two, (), z, part, row, [cells[c] + out[c] for c in range(3)])
                    put(rate_one, (kept,), z, part, row, out)

                evaluate(node_one.at[kept], aux, halo, use)

            @pl.when((me - count >= 0) & (sweep > 0))
            def _():
                def use(row, part, z, out, cells):
                    add = get(extra, (kept - 1,), z, part, row)
                    put(node_two, (), z, part, row, [cells[c] + out[c] + add[c] for c in range(3)])
                    put(rate_one, (kept,), z, part, row, out)

                evaluate(node_one.at[kept], aux, halo, use)

            pl.when((me - count == -1) & (sweep + 1 < ITERS))(lambda: load_start(node_two))

            @pl.when((count == 0) & (sweep + 1 < ITERS))
            def _():
                def use(row, part, z, out, cells):
                    put(rate_two, (), z, part, row, out)

                evaluate(node_two, aux, halo - 1, use)

            @pl.when((count > 0) & (me - count >= -1) & (sweep + 1 < ITERS))
            def _():
                def use(row, part, z, out, cells):
                    old = get(rate_zero, (kept + 1,), z, part, row)
                    mid = get(rate_one, (kept + 1,), z, part, row)
                    far = get(rate_two, (), z, part, row)
                    put(node_one, (kept + 1,), z, part, row, [
                        cells[c] + out[c] + (1.0 / 12.0) * (8.0 * mid[c] - 7.0 * old[c] - far[c])
                        for c in range(3)])
                    put(extra, (kept,), z, part, row, [
                        (1.0 / 12.0) * ((far[c] - old[c]) + 4.0 * (far[c] - mid[c]))
                        for c in range(3)])
                    put(rate_zero, (kept + 1,), z, part, row, out)
                    put(rate_two, (), z, part, row, out)

                evaluate(node_two, aux, halo - 1, use)

            return carry

        return lax.fori_loop(0, ITERS - sweep, one_slice, carry)

    lax.fori_loop(0, ITERS, sweep_slices, 0)
    assemble(node_two, end_ref, end_hbm, sems.at[5], order_ref)
    pltpu.make_async_copy(guess_ref, guess_hbm, sems.at[4]).wait()
    pltpu.make_async_copy(end_ref, end_hbm, sems.at[5]).wait()


def compute(index, table, fields, interpret=False):
    field = (3, 4, PARTS, ROWS, 128)
    smem = pl.BlockSpec(memory_space=pltpu.SMEM)
    return pl.pallas_call(
        compute_kernel,
        name="llg",
        out_shape=[jax.ShapeDtypeStruct((3, 4, 64, 256), jnp.float32)] * 2,
        in_specs=[smem, smem, pl.BlockSpec(memory_space=pltpu.HBM)],
        out_specs=[pl.BlockSpec(memory_space=pltpu.HBM)] * 2,
        scratch_shapes=[
            pltpu.VMEM((3, 4, 64, 256), jnp.float32),
            pltpu.VMEM((3, 4, 64, 256), jnp.float32),
            pltpu.VMEM(field, jnp.float32),
            pltpu.VMEM(field, jnp.float32),
            pltpu.VMEM((4,) + field, jnp.float32),
            pltpu.VMEM((3,) + field, jnp.float32),
            pltpu.VMEM((4,) + field, jnp.float32),
            pltpu.VMEM((4,) + field, jnp.float32),
            pltpu.VMEM(field, jnp.float32),
            pltpu.VMEM(field, jnp.float32),
            pltpu.VMEM(field, jnp.float32),
        ] + [pltpu.VMEM(field[1:], jnp.float32)] * 5 + [
            pltpu.VMEM((256, 256), jnp.bfloat16), pltpu.SemaphoreType.DMA((6,))],
        compiler_params=pltpu.CompilerParams(vmem_limit_bytes=62 * 1024 * 1024),
        interpret=interpret,
    )(index, table, fields)


def halo_kernel(start_hbm, demag_hbm, region_hbm, out_ref, start_ref, demag_ref, region_ref, order_ref, own, down, up, side_out, side_in, corner_out, corner_in, corner,
                send_sems, recv_sems, local_sems):
    gx, gy, tm = lax.axis_index("gx"), lax.axis_index("gy"), lax.axis_index("tm")
    count = lax.axis_size("gx")
    after = {"gx": lax.rem(gx + 1, count)}
    before = {"gx": lax.rem(gx + count - 1, count)}
    across = {"tm": tm + 1 - 2 * lax.rem(tm, 2), "gy": 1 - gy}
    loads = [pltpu.make_async_copy(source, target, local_sems.at[3 + k]) for k, (source, target) in enumerate(
        ((start_hbm, start_ref), (demag_hbm, demag_ref), (region_hbm, region_ref)))]
    for copy in loads:
        copy.start()
    barrier = pltpu.get_barrier_semaphore()
    for device in (after, before, across):
        pl.semaphore_signal(barrier, inc=1, device_id=device, device_id_type=MESH)

    upside_down = 7 - lax.broadcasted_iota(jnp.int32, (8, 128), 0)
    lane = lanes()

    def flip(value):
        return jnp.take_along_axis(value, upside_down, axis=0)

    def load(f, z):
        if f < 3:
            return 0.5 * start_ref[f, z]
        if f < 6:
            return STEP * demag_ref[f - 3, z]
        return region_ref[z].astype(jnp.float32)

    def quarters(a, b, c, d):
        return jnp.where(lane < 64, jnp.where(lane < 32, a, b), jnp.where(lane < 96, c, d))

    def piece(values, row, part):
        return values[row:row + 8, 128 * part:128 * part + 128]

    def stage_sides(z, carry):
        for f in range(7):
            tile = load(f, z)
            for k in range(4):
                a = [piece(tile, 8 * k, part) for part in range(2)]
                b = [flip(piece(tile, 56 - 8 * k, part)) for part in range(2)]
                side_out[f, z, 8 * k:8 * k + 8, :] = quarters(a[0], pltpu.roll(b[0], 32, 1), pltpu.roll(b[1], 96, 1), a[1])
        return carry

    def stage_rows(z, carry):
        for f in range(7):
            tile = load(f, z)
            if f < 6:
                halves = permuted(tile, order_ref[...])
            else:
                halves = jnp.dot(tile.astype(jnp.bfloat16), order_ref[...], preferred_element_type=jnp.float32)
            for k in range(4):
                rows = slice(8 * k, 8 * k + 8)
                for part in range(2):
                    own[f, z, part, rows, :] = piece(halves, 8 * k, part)
                    own[f, z, part + 2, rows, :] = flip(piece(halves, 56 - 8 * k, part))
            for k in range(3):
                rows = slice(8 * k, 8 * k + 8)
                for part in range(2):
                    down[f, z, part, rows, :] = piece(halves, 40 + 8 * k, part)
                    up[f, z, part, rows, :] = flip(piece(halves, 16 - 8 * k, part))
        return carry

    def send(number, source, target, device):
        copy = pltpu.make_async_remote_copy(source, target, send_sems.at[number], recv_sems.at[number],
                                            device_id=device, device_id_type=MESH)
        copy.start()
        return copy

    for copy in loads:
        copy.wait()
    lax.fori_loop(0, 4, stage_sides, 0)
    pl.semaphore_wait(barrier, 3)
    near, far = slice(0, HALO), slice(HALO, 32)
    sides = [send(0, side_out.at[:, :, near, :], side_in.at[:, :, near, :], across)]
    order_ref[...] = spread(0)
    lax.fori_loop(0, 4, stage_rows, 0)
    edge, inner = slice(FIRST, FIRST + HALO), slice(FIRST + HALO, LAST)
    edges = [send(2, down, out_ref.at[:, :, 0:2, edge, :], after), send(3, up, out_ref.at[:, :, 2:4, edge, :], before)]
    middle = pltpu.make_async_copy(own, out_ref.at[:, :, 0:4, inner, :], local_sems.at[0])
    middle.start()
    sides[0].wait_recv()
    sides.append(send(1, side_out.at[:, :, far, :], side_in.at[:, :, far, :], across))

    def turn(pair, carry):
        for f in range(7):
            for k in range(3):
                rows = slice(8 * k, 8 * k + 8)
                back = slice(16 - 8 * k, 24 - 8 * k)
                one = flip(side_in[f, pair, back, :])
                two = flip(side_in[f, pair + 2, back, :])
                one_left, one_right = pltpu.roll(one, 96, 1), pltpu.roll(one, 32, 1)
                two_left, two_right = pltpu.roll(two, 96, 1), pltpu.roll(two, 32, 1)
                corner_out[0, f, pair, rows, :] = quarters(one_left, two_left, two_right, one_right)
                corner_out[1, f, pair, rows, :] = quarters(two_right, one_right, one_left, two_left)
        return carry

    lax.fori_loop(0, 2, turn, 0)
    corners = [send(4, corner_out.at[0], corner_in.at[0], after), send(5, corner_out.at[1], corner_in.at[1], before)]
    sides[1].wait_recv()
    strip = pltpu.make_async_copy(side_in, out_ref.at[:, :, 4, inner, :], local_sems.at[1])
    strip.start()
    corners[0].wait_recv()
    corners[1].wait_recv()
    mid = (lane >= 32) & (lane < 96)

    def unpack(pair, carry):
        for f in range(7):
            for k in range(3):
                rows = slice(8 * k, 8 * k + 8)
                upper, lower = corner_in[0, f, pair, rows, :], corner_in[1, f, pair, rows, :]
                corner[f, pair, rows, :] = jnp.where(mid, lower, upper)
                corner[f, pair + 2, rows, :] = pltpu.roll(jnp.where(mid, upper, lower), 64, 1)
        return carry

    lax.fori_loop(0, 2, unpack, 0)
    last = pltpu.make_async_copy(corner, out_ref.at[:, :, 4, edge, :], local_sems.at[2])
    last.start()
    for copy in edges:
        copy.wait()
    for copy in sides + corners:
        copy.wait_send()
    middle.wait()
    strip.wait()
    last.wait()


def gather_halo(start_field, demag_field, region_map):
    hbm = pl.BlockSpec(memory_space=pltpu.HBM)
    return pl.pallas_call(
        halo_kernel,
        name="halo",
        out_shape=jax.ShapeDtypeStruct((7, 4, PARTS, ROWS, 128), jnp.float32),
        in_specs=[hbm] * 3,
        out_specs=hbm,
        scratch_shapes=[
            pltpu.VMEM((3, 4, 64, 256), jnp.float32),
            pltpu.VMEM((3, 4, 64, 256), jnp.float32),
            pltpu.VMEM((4, 64, 256), jnp.int32),
            pltpu.VMEM((256, 256), jnp.bfloat16),
            pltpu.VMEM((7, 4, 4, 32, 128), jnp.float32),
            pltpu.VMEM((7, 4, 2, HALO, 128), jnp.float32),
            pltpu.VMEM((7, 4, 2, HALO, 128), jnp.float32),
            pltpu.VMEM((7, 4, 32, 128), jnp.float32),
            pltpu.VMEM((7, 4, 32, 128), jnp.float32),
            pltpu.VMEM((2, 7, 2, HALO, 128), jnp.float32),
            pltpu.VMEM((2, 7, 2, HALO, 128), jnp.float32),
            pltpu.VMEM((7, 4, HALO, 128), jnp.float32),
            pltpu.SemaphoreType.DMA((6,)),
            pltpu.SemaphoreType.DMA((6,)),
            pltpu.SemaphoreType.DMA((6,)),
        ],
        compiler_params=pltpu.CompilerParams(
            collective_id=0, has_side_effects=True, vmem_limit_bytes=62 * 1024 * 1024),
    )(start_field, demag_field, region_map)


def on_device(start_field, demag_field, region_map, material_table):
    fields = gather_halo(start_field, demag_field, region_map)
    index = lax.axis_index("tm").astype(jnp.int32)[None]
    end, guess = compute(index, material_table, fields)
    return end[None], guess[None]


def solution(mesh):
    placed = (P(None, None, "gx", "gy"), P(None, None, "gx", "gy"), P(None, "gx", "gy"), P())
    return jax.shard_map(
        on_device,
        mesh=mesh,
        in_specs=placed,
        out_specs=(P("tm", None, None, "gx", "gy"), P("tm", None, None, "gx", "gy")),
        check_vma=False,
    )
```
